32 devices in a mesh: ctx: 8 (over y, x, core), chan: 4 (over z).
Axes of the slice: x: 2, y: 2, z: 4, core: 2. Of those that a mesh axis runs over, the one named last changes fastest.
Arguments:
- x_gate: bfloat16 [1024, 4096], P('ctx', 'chan'), may hold values from -6 to 6
- x_key: bfloat16 [1024, 4096], P('ctx', 'chan'), may hold values from -6 to 6
- x_value: bfloat16 [1024, 4096], P('ctx', 'chan'), may hold values from -6 to 6
- filters: bfloat16 [1024, 256], P('ctx', 'chan'), may hold values from -1.1 to 1.1
- bias: float32 [4096], P('chan'), may hold values from 0.5 to 1.5
- w_out: bfloat16 [4096, 4096], P('chan'), may hold values from -0.09375 to 0.09375
Outputs:
- mixed: bfloat16 [1024, 4096], P('ctx', 'chan')
The draws below stay inside these ranges and needn't reach their ends.
All inputs are finite; a program needn't handle non-finite values.
Results may differ from the reference program's by a relative error of at most 0.014.
Values may be sent and summed in bfloat16 or wider, within the bound.
No kernel may reach another device: no remote copies, remote signals or barrier semaphores. Data moves between devices by JAX's collectives and lax.ppermute only.
A program may use at most 64 MiB of HBM per device.

```python
import math
import jax
import jax.numpy as jnp
from jax import lax

D = 4096
GS = 16
GROUPS = 256
SEQ = 1024
N_CHAN = 4


def draw_filters(key, part):
    key_rate = jax.random.fold_in(key, 11)
    key_taps = jax.random.fold_in(key, 23)
    log_tau = jax.random.uniform(key_rate, (GROUPS,), jnp.float32, math.log(30.0), math.log(4.0 * SEQ))
    tau = jnp.exp(log_tau)
    steps = jnp.arange(SEQ, dtype=jnp.float32)[:, None]
    envelope = jnp.exp(-steps / tau[None, :]) * jnp.sqrt(2.0 / jnp.minimum(tau, 1.0 * SEQ))[None, :]
    rough = jnp.clip(jax.random.normal(key_taps, (SEQ, GROUPS), jnp.float32), -4.0, 4.0)
    return (rough * envelope).astype(jnp.bfloat16)


def levels(stream_key, dims, pieces, smallest, largest):
    factor_of, own = 1.0, jax.random.fold_in(stream_key, 6)
    for axis_at, parts in pieces:
        heights = jnp.exp(jax.random.uniform(jax.random.fold_in(own, axis_at), (parts,), jnp.float32, smallest / len(pieces), largest / len(pieces)))
        factor_of = factor_of * jnp.repeat(heights, dims[axis_at] // parts).reshape([-1 if axis == axis_at else 1 for axis in range(len(dims))])
    return factor_of


def gaussian(rng, shape, spread, limit, cuts=(), kind=jnp.bfloat16):
    drawn = spread * jax.random.normal(rng, shape, jnp.float32)
    if cuts:
        drawn = drawn * levels(rng, shape, cuts, -0.22, 0.18)
    return jnp.clip(drawn, -limit, limit).astype(kind)


def setup_inputs(seed: int = 0) -> dict:
    arg_keys = jax.random.split(jax.random.key(seed), 7)
    return {
        "x_gate": gaussian(arg_keys[0], (SEQ, D), 1.0, 6.0, ((0, 8), (1, 4))),
        "x_key": gaussian(arg_keys[1], (SEQ, D), 1.0, 6.0, ((0, 8), (1, 4))),
        "x_value": gaussian(arg_keys[2], (SEQ, D), 1.0, 6.0, ((0, 8), (1, 4))),
        "filters": draw_filters(jax.random.fold_in(arg_keys[6], 71), 0),
        "bias": jnp.clip(0.5 + 1.0 * jax.random.uniform(arg_keys[4], (D,), jnp.float32) ** levels(arg_keys[4], (D,), ((0, 4),), -0.2, 0.2), 0.5, 1.5),
        "w_out": gaussian(arg_keys[5], (D, D), D ** -0.5, 0.09375, ((0, 4),)),
    }


def reference(x_gate, x_key, x_value, filters, bias, w_out):
    z = (x_key.astype(jnp.float32) * x_value.astype(jnp.float32)).astype(jnp.bfloat16).astype(jnp.float32)
    taps = jnp.repeat(filters.astype(jnp.float32), GS, axis=1)
    length = 2 * SEQ
    spec = jnp.fft.rfft(z, length, axis=0) * jnp.fft.rfft(taps, length, axis=0)
    conv = jnp.fft.irfft(spec, length, axis=0)[:SEQ].astype(jnp.float32)
    gated = (x_gate.astype(jnp.float32) * (conv + bias[None, :] * z)).astype(jnp.bfloat16)
    width = D // N_CHAN
    total = jnp.zeros((SEQ, D), jnp.float32)
    for block in range(N_CHAN):
        part = jnp.dot(gated[:, block * width:(block + 1) * width], w_out[block * width:(block + 1) * width], preferred_element_type=jnp.float32)
        part = lax.optimization_barrier(part.astype(jnp.bfloat16))
        total = total + part.astype(jnp.float32)
    return total.astype(jnp.bfloat16)
```

```python
import functools

import jax
import jax.numpy as jnp
from jax import lax
from jax.experimental import pallas as pl
from jax.experimental.pallas import tpu as pltpu
from jax.sharding import PartitionSpec as P

F32 = jnp.float32
BF16 = jnp.bfloat16


def pad_rows(rows):
    return -(-rows // 16) * 16


def pack_kernel(parts, key_ref, value_ref, taps_ref, out_ref):
    channels = key_ref.shape[1] // parts
    groups = taps_ref.shape[0] // parts
    tokens = key_ref.shape[0]
    taps = taps_ref[...].astype(F32)
    filler = jnp.zeros((pad_rows(groups) - groups, tokens), F32)
    for part in range(parts):
        lanes = slice(part * channels, (part + 1) * channels)
        z = (key_ref[:, lanes].astype(F32) * value_ref[:, lanes].astype(F32)).astype(BF16)
        out_ref[part, :channels, :] = z.T
        mine = taps[part * groups : (part + 1) * groups]
        if filler.shape[0]:
            mine = jnp.concatenate([mine, filler], axis=0)
        out_ref[part, channels:, :] = mine.astype(BF16)


def pack(x_key, x_value, taps, parts):
    tokens, width = x_key.shape
    rows = width // parts + pad_rows(taps.shape[0] // parts)
    return pl.pallas_call(
        functools.partial(pack_kernel, parts),
        out_shape=jax.ShapeDtypeStruct((parts, rows, tokens), BF16),
        name="pack",
    )(x_key, x_value, taps)


def conv_kernel(size, groups, in_ref, out_ref):
    blocks, _, tokens = in_ref.shape
    channels = size * groups
    row = lax.broadcasted_iota(jnp.int32, (tokens, tokens), 0)
    col = lax.broadcasted_iota(jnp.int32, (tokens, tokens), 1)
    later = col >= row
    for group in range(groups):
        tiles = []
        before = jnp.zeros((tokens, tokens), F32)
        for block in range(blocks):
            taps = in_ref[block, channels + group : channels + group + 1, :].astype(F32)
            spread = jnp.broadcast_to(taps, (tokens, tokens))
            rolled = pltpu.roll(spread, 0, 1, stride=1, stride_axis=0)
            tiles.append(jnp.where(later, rolled, before).astype(BF16))
            before = rolled
        toeplitz = jnp.concatenate(tiles, axis=1)
        source = in_ref[:, group * size : (group + 1) * size, :].reshape(blocks * size, tokens)
        product = jnp.dot(source, toeplitz, preferred_element_type=F32)
        for block in range(blocks):
            total = product[:size, block * tokens : (block + 1) * tokens]
            for src in range(1, block + 1):
                lag = block - src
                total = total + product[
                    src * size : (src + 1) * size, lag * tokens : (lag + 1) * tokens
                ]
            out_ref[block, group * size : (group + 1) * size, :] = total.astype(BF16)


def conv(received, size, groups):
    blocks, _, tokens = received.shape
    return pl.pallas_call(
        functools.partial(conv_kernel, size, groups),
        out_shape=jax.ShapeDtypeStruct((blocks, size * groups, tokens), BF16),
        name="conv",
    )(received)


def gate_kernel(which_ref, conv_ref, gate_ref, key_ref, value_ref, bias_ref, w_ref, gated_ref, part_ref):
    parts, channels, _ = conv_ref.shape
    for part in range(parts):
        lanes = slice(part * channels, (part + 1) * channels)
        z = (key_ref[:, lanes].astype(F32) * value_ref[:, lanes].astype(F32)).astype(BF16)
        mixed = conv_ref[part].T.astype(F32) + bias_ref[:, lanes] * z.astype(F32)
        gated_ref[:, lanes] = (gate_ref[:, lanes].astype(F32) * mixed).astype(BF16)
    part_ref[...] = jnp.dot(gated_ref[...], w_ref[...], preferred_element_type=F32).astype(BF16)


def gate_and_project(which, conved, x_gate, x_key, x_value, bias, w_out, width):
    tokens, depth = x_gate.shape
    full = lambda shape: pl.BlockSpec(shape, lambda i, which: (0,) * len(shape))
    grid_spec = pltpu.PrefetchScalarGridSpec(
        num_scalar_prefetch=1,
        grid=(1,),
        in_specs=[
            full(conved.shape),
            full(x_gate.shape),
            full(x_key.shape),
            full(x_value.shape),
            full((1, depth)),
            pl.BlockSpec((depth, width), lambda i, which: (0, which[0])),
        ],
        out_specs=[full((tokens, depth)), full((tokens, width))],
    )
    return pl.pallas_call(
        gate_kernel,
        grid_spec=grid_spec,
        out_shape=[
            jax.ShapeDtypeStruct((tokens, depth), BF16),
            jax.ShapeDtypeStruct((tokens, width), BF16),
        ],
        name="gate",
    )(which, conved, x_gate, x_key, x_value, bias.reshape(1, depth), w_out)


def project_kernel(which_ref, gated_ref, w_ref, part_ref):
    part_ref[0] = jnp.dot(gated_ref[...], w_ref[...], preferred_element_type=F32).astype(BF16)


def project(which, gated, w_out, width):
    tokens, depth = gated.shape
    steps = which.shape[0]
    grid_spec = pltpu.PrefetchScalarGridSpec(
        num_scalar_prefetch=1,
        grid=(steps,),
        in_specs=[
            pl.BlockSpec((tokens, depth), lambda i, which: (0, 0)),
            pl.BlockSpec((depth, width), lambda i, which: (0, which[i])),
        ],
        out_specs=pl.BlockSpec((1, tokens, width), lambda i, which: (i, 0, 0)),
    )
    return pl.pallas_call(
        project_kernel,
        grid_spec=grid_spec,
        out_shape=jax.ShapeDtypeStruct((steps, tokens, width), BF16),
        name="project",
    )(which, gated, w_out)


def local(x_gate, x_key, x_value, filters, bias, w_out):
    tokens, depth = x_key.shape
    parts = lax.axis_size("ctx")
    planes = lax.axis_size("chan")
    width = w_out.shape[1] // planes
    size = depth // filters.shape[1]
    groups = filters.shape[1] // parts

    sent = pack(x_key, x_value, filters.T, parts)
    received = lax.all_to_all(sent, "ctx", split_axis=0, concat_axis=0, tiled=True)
    conved = conv(received, size, groups)
    conved = lax.all_to_all(conved, "ctx", split_axis=0, concat_axis=0, tiled=True)

    me = lax.axis_index("chan")
    if planes != 4:
        gated, first = gate_and_project(
            jnp.zeros((1,), jnp.int32), conved, x_gate, x_key, x_value, bias, w_out, width
        )
        rest = project(jnp.arange(1, planes, dtype=jnp.int32), gated, w_out, width)
        whole = jnp.concatenate([first[None], rest], axis=0)
        return lax.psum_scatter(whole, "chan", scatter_dimension=0, tiled=False)

    inner = (me == 1) | (me == 2)
    order = jnp.array([[3, 2, 1, 0], [0, 2, 3, 1], [3, 1, 0, 2], [0, 1, 2, 3]], jnp.int32)
    order = lax.dynamic_index_in_dim(order, me, 0, keepdims=False)
    gated, near = gate_and_project(
        order[:1], conved, x_gate, x_key, x_value, bias, w_out, width
    )
    from_near = lax.ppermute(near, "chan", [(0, 1), (1, 0), (2, 3), (3, 2)])
    second = project(order[1:2], gated, w_out, width)[0]
    from_middle = lax.ppermute(second, "chan", [(1, 2), (2, 1)])
    from_far = lax.ppermute(second, "chan", [(0, 2), (3, 1)])
    last = project(order[2:], gated, w_out, width)
    relay = (last[0].astype(F32) + jnp.where(inner, from_near.astype(F32), 0.0)).astype(BF16)
    from_relay = lax.ppermute(relay, "chan", [(0, 1), (1, 3), (3, 2), (2, 0)])
    total = last[1].astype(F32) + jnp.where(inner, 0.0, from_near.astype(F32))
    total = total + from_middle.astype(F32) + from_far.astype(F32) + from_relay.astype(F32)
    return total.astype(BF16)


def solution(mesh):
    placed = (
        P("ctx", "chan"),
        P("ctx", "chan"),
        P("ctx", "chan"),
        P("ctx", "chan"),
        P("chan"),
        P("chan", None),
    )
    return jax.shard_map(
        local, mesh=mesh, in_specs=placed, out_specs=P("ctx", "chan"), check_vma=False
    )
```
